256 devices in a mesh: gz: 16 (over y_lo, x, core), gy: 16 (over z, y_hi).
Axes of the slice: x: 4, y: 4 (y_hi: 2, y_lo: 2; y = y_hi * 2 + y_lo), z: 8, core: 2. Of those that a mesh axis runs over, the one named last changes fastest.
Arguments:
- electric: float32 [3, 256, 128, 256], P(None, 'gz', 'gy'), may hold values from -6 to 6
- magnetic: float32 [3, 256, 128, 256], P(None, 'gz', 'gy'), may hold values from -6 to 6
- material: int32 [256, 128, 256], P('gz', 'gy'), may hold values from 0 to 15
- incoming: int32 [32, 128, 256], P(None, 'gy'), may hold values from 0 to 15
- shift_flags: int32 [8], replicated, may hold values from 0 to 1, as said below
- eps_table: float32 [16], replicated, may hold values from 1 to 6
- sigma_table: float32 [16], replicated, may hold values from 0 to 1
- kerr_table: float32 [16], replicated, may hold values from 0.05 to 0.5
Outputs:
- electric_out: float32 [3, 256, 128, 256], P(None, 'gz', 'gy')
- magnetic_out: float32 [3, 256, 128, 256], P(None, 'gz', 'gy')
The draws below stay inside these ranges and needn't reach their ends.
Inputs may be any that keep to these rules, and one draw needn't show every extreme that they name: `shift_flags`: exactly 4 entries are 1, the others 0.
All inputs are finite; a program needn't handle non-finite values.
Results may differ from the reference program's by a relative error of at most 0.00002.
Values sent between devices are 32-bit elements; how exact they have to be, the bound alone decides.
A program may use at most 64 MiB of HBM per device.

```python
import math
import jax
import jax.numpy as jnp
from jax import lax

NX = 256
STEPS = 8
SHIFTS = 4
SHIFT = 8
MAT = 16
NZ = 256
NY = 128


def draw_shift_flags(key, part):
    ranking = jax.random.permutation(key, STEPS)
    return (ranking < SHIFTS).astype(jnp.int32)


def set_ends(drawn, key, smallest, top_value):
    dims = drawn.shape
    place = [jax.random.randint(jax.random.fold_in(key, axis), (), 0, dims[axis]) for axis in range(len(dims))]
    drawn = drawn.at[tuple(place)].set(smallest)
    longest = dims.index(max(dims))
    place[longest] = (place[longest] + 1) % dims[longest]
    return drawn.at[tuple(place)].set(top_value)


def levels(stream_key, extent, pieces, smallest, top_value):
    level = 1.0
    for position, blocks in pieces:
        heights = jax.random.uniform(jax.random.fold_in(jax.random.fold_in(stream_key, 6), position), (blocks,), jnp.float32, smallest / len(pieces), top_value / len(pieces))
        level = level * jnp.repeat(jnp.exp(heights), extent[position] // blocks).reshape((-1,) + (1,) * (len(extent) - 1 - position))
    return level


def gaussian(stream_key, shape, deviation, most, split=(), held_as=jnp.bfloat16):
    result = jax.random.normal(stream_key, shape, jnp.float32) * deviation
    if len(split) > 0:
        result = levels(stream_key, shape, split, -0.22, 0.18) * result
    return jnp.clip(result, min=-most, max=most).astype(held_as)


def setup_inputs(seed: int = 0) -> dict:
    streams_of = jax.random.split(jax.random.key(seed), 9)
    electric = gaussian(streams_of[0], (3, NZ, NY, NX), 1.0, 6.0, ((1, 16), (2, 16)), jnp.float32)
    magnetic = gaussian(streams_of[1], (3, NZ, NY, NX), 1.0, 6.0, ((1, 16), (2, 16)), jnp.float32)
    material = set_ends(jax.random.randint(streams_of[2], (NZ, NY, NX), 0, MAT), jax.random.fold_in(streams_of[2], 1), 0, MAT - 1).astype(jnp.int32)
    incoming = set_ends(jax.random.randint(streams_of[3], (SHIFTS * SHIFT, NY, NX), 0, MAT), jax.random.fold_in(streams_of[3], 1), 0, MAT - 1).astype(jnp.int32)
    shift_flags = draw_shift_flags(jax.random.fold_in(streams_of[8], 71), 0)
    eps_table = jnp.clip(jnp.exp(jax.random.uniform(streams_of[5], (MAT,), jnp.float32, math.log(1.0), math.log(6.0))), 1.0, 6.0)
    sigma_table = jnp.clip(jax.random.uniform(streams_of[6], (MAT,), jnp.float32, 0.0, 1.0), 0.0, 1.0)
    kerr_table = jnp.clip(jax.random.uniform(streams_of[7], (MAT,), jnp.float32, 0.05, 0.5), 0.05, 0.5)
    return {"electric": electric, "magnetic": magnetic, "material": material, "incoming": incoming, "shift_flags": shift_flags, "eps_table": eps_table, "sigma_table": sigma_table, "kerr_table": kerr_table}


courant_number = 0.5


def forward_diff(field, axis_no):
    length = field.shape[axis_no]
    shifted = jnp.concatenate([lax.slice_in_dim(field, 1, length, axis=axis_no), jnp.zeros_like(lax.slice_in_dim(field, 0, 1, axis=axis_no))], axis=axis_no)
    return shifted - field


def backward_diff(field, axis_no):
    length = field.shape[axis_no]
    shifted = jnp.concatenate([jnp.zeros_like(lax.slice_in_dim(field, 0, 1, axis=axis_no)), lax.slice_in_dim(field, 0, length - 1, axis=axis_no)], axis=axis_no)
    return field - shifted


def curl_parts(vector, differ):
    part_x = differ(vector[2], 1) - differ(vector[1], 0)
    part_y = differ(vector[0], 0) - differ(vector[2], 2)
    part_z = differ(vector[1], 2) - differ(vector[0], 1)
    return jnp.stack([part_x, part_y, part_z])


def e_update(electric, curl_h, coefs):
    square = electric[0] * electric[0] + electric[1] * electric[1] + electric[2] * electric[2]
    permit = coefs[0] + coefs[2] * square
    damping = 0.5 * coefs[1] / permit
    return ((1.0 - damping) * electric + (courant_number / permit) * curl_h) / (1.0 + damping)


def lookup(id_map, eps_table, sigma_table, kerr_table):
    return jnp.stack([eps_table[id_map], sigma_table[id_map], kerr_table[id_map]])


def reference(electric, magnetic, material, incoming, shift_flags, eps_table, sigma_table, kerr_table):
    coefs = lookup(material, eps_table, sigma_table, kerr_table)
    done_count = jnp.int32(0)
    for step_no in range(STEPS):
        shift_on = shift_flags[step_no] == 1
        new_ids = lax.dynamic_slice_in_dim(incoming, (done_count * SHIFT).astype(jnp.int32), SHIFT, 0)
        new_coefs = lookup(new_ids, eps_table, sigma_table, kerr_table)
        zero_planes = jnp.zeros((3, SHIFT, NY, NX), jnp.float32)
        electric = jnp.where(shift_on, jnp.concatenate([electric[:, SHIFT:], zero_planes], 1), electric)
        magnetic = jnp.where(shift_on, jnp.concatenate([magnetic[:, SHIFT:], zero_planes], 1), magnetic)
        coefs = jnp.where(shift_on, jnp.concatenate([coefs[:, SHIFT:], new_coefs], 1), coefs)
        done_count = done_count + shift_flags[step_no]
        magnetic = magnetic - courant_number * curl_parts(electric, forward_diff)
        electric = e_update(electric, curl_parts(magnetic, backward_diff), coefs)
    return electric, magnetic
```

```python
import jax
import jax.numpy as jnp
from jax import lax
from jax.experimental import pallas as pl
from jax.experimental.pallas import tpu as pltpu
from jax.sharding import PartitionSpec as P

STEPS = 8
SHIFT = 8
HALF = 4
MESH = pl.DeviceIdType.MESH
F32 = jnp.float32


def kernel(
    flags, eps_t, sig_t, ker_t, e_in, h_in, mat, inc,
    o_e, o_h,
    fa, fb, fc, fo, ca, cia, cb, cib, ma, face,
    sm, rm, si, ri, sb1, rb1, xb, rx, sb2, rb2, ss, rs,
):
    nz_dev = lax.axis_size("gz")
    ny_dev = lax.axis_size("gy")
    g = lax.axis_index("gz")
    y = lax.axis_index("gy")
    pz = e_in.shape[1]
    nx = e_in.shape[3]
    slots = nz_dev * pz
    ext = pz + 2 * HALF
    tile = (8, nx)

    def zdev(d):
        return (lax.rem(g + d + nz_dev, nz_dev), y)

    def ydev(d):
        return (g, lax.rem(y + d + ny_dev, ny_dev))

    barrier = pltpu.get_barrier_semaphore()
    partners = [zdev(1), zdev(-1), ydev(1), ydev(-1), zdev(2), zdev(-2)]
    for dev in partners:
        pl.semaphore_signal(barrier, inc=1, device_id=dev, device_id_type=MESH)

    row = lax.broadcasted_iota(jnp.int32, tile, 0)
    lane = lax.broadcasted_iota(jnp.int32, tile, 1)
    low_rows = row < HALF
    first_lane = lane == 0
    last_lane = lane == nx - 1
    at_edge = y == 0
    up_cut = jnp.where((row == HALF - 1) & at_edge, 0.0, 1.0).astype(F32)
    down_cut = jnp.where((row == HALF) & at_edge, 0.0, 1.0).astype(F32)
    face_ok = jnp.where(at_edge, 0.0, 1.0).astype(F32)

    def half_turn(v):
        return pltpu.roll(v, HALF, 0)

    def remote(src, dst, sem_no, dev):
        return pltpu.make_async_remote_copy(
            src, dst, ss.at[sem_no], rs.at[sem_no], device_id=dev, device_id_type=MESH
        )

    for c in range(3):
        fa[c, HALF : HALF + pz] = e_in[c]
        fa[3 + c, HALF : HALF + pz] = h_in[c]
    ma[HALF : HALF + pz] = mat[...]
    for i in range(inc.shape[0] // 2):
        si[i] = jnp.where(low_rows, half_turn(inc[2 * i]), inc[2 * i + 1])

    pl.semaphore_wait(barrier, len(partners))

    top = pl.ds(pz - HALF, HALF)
    bottom = pl.ds(0, HALF)
    lo_halo = pl.ds(0, HALF)
    hi_halo = pl.ds(HALF + pz, HALF)
    first = [
        remote(e_in.at[:, top], fa.at[pl.ds(0, 3), lo_halo], 0, zdev(1)),
        remote(h_in.at[:, top], fa.at[pl.ds(3, 3), lo_halo], 1, zdev(1)),
        remote(mat.at[top], ma.at[lo_halo], 2, zdev(1)),
        remote(e_in.at[:, bottom], fa.at[pl.ds(0, 3), hi_halo], 3, zdev(-1)),
        remote(h_in.at[:, bottom], fa.at[pl.ds(3, 3), hi_halo], 4, zdev(-1)),
        remote(mat.at[bottom], ma.at[hi_halo], 5, zdev(-1)),
    ]
    for copy in first:
        copy.start()
    inc_copy = remote(si, ri, 6, ydev(1))
    inc_copy.start()

    def lookup(ids):
        out = [jnp.zeros(tile, F32) for _ in range(3)]
        for t in range(eps_t.shape[0]):
            here = ids == t
            for i, tab in enumerate((eps_t, sig_t, ker_t)):
                out[i] = jnp.where(here, tab[t], out[i])
        return out[0], 0.5 * out[1], out[2]

    def slot_of(p):
        return lax.rem(g * pz - HALF + p + slots, slots)

    def put(ref, p, values):
        for i in range(3):
            ref[i, p] = values[i]

    def inc_plane(p):
        return lax.rem(slot_of(p), inc.shape[0])

    def own_incoming(p, carry):
        put(cia, p, lookup(inc[inc_plane(p)]))
        return carry

    lax.fori_loop(0, ext, own_incoming, 0)

    for copy in first:
        copy.wait()

    for i in range(ext // 2):
        sm[i] = jnp.where(low_rows, half_turn(ma[2 * i]), ma[2 * i + 1])
    mat_copy = remote(sm, rm, 7, ydev(1))
    mat_copy.start()

    def own_material(p, carry):
        put(ca, p, lookup(ma[p]))
        return carry

    lax.fori_loop(0, ext, own_material, 0)

    counts = []
    total = jnp.int32(0)
    for s in range(STEPS):
        total = total + flags[s]
        counts.append(total)

    def x_up(v):
        return jnp.where(last_lane, 0.0, pltpu.roll(v, nx - 1, 1))

    def x_down(v):
        return jnp.where(first_lane, 0.0, pltpu.roll(v, 1, 1))

    def level(step, k, src, dst, off, coef, coef_inc, inverted, shifted, use_face):
        if inverted:
            h_rows = (row >= HALF - 1 - k) & (row < HALF + k)
            e_rows = (row >= HALF - 1 - k) & (row < HALF + 1 + k)
        else:
            h_rows = (row >= k) & (row < 2 * HALF - 1 - k)
            e_rows = (row >= k + 1) & (row < 2 * HALF - 1 - k)
        count = counts[step]
        cut = count * SHIFT

        def keep(p):
            slot = slot_of(p)
            fresh = (flags[step] == 1) & (slot < cut) & (slot >= cut - SHIFT)
            return jnp.where(fresh, 0.0, 1.0).astype(F32)

        def y_up(v):
            v = pltpu.roll(v, 7, 0)
            return v * up_cut if shifted else v

        def y_down(v, face_no, p):
            v = pltpu.roll(v, 1, 0)
            if shifted:
                v = v * down_cut
            if use_face:
                v = jnp.where(row == 0, face[face_no, p - HALF], v)
            return v

        def magnetic(p):
            stay = keep(p)
            above = jnp.where(slot_of(p) == lax.rem(cut + slots - 1, slots), 0.0, 1.0).astype(F32) * keep(p + 1)
            raw = [src[c, p] for c in range(3)]
            ex, ey, ez = (v * stay for v in raw)
            ux, uy = (src[c, p + 1] * above for c in range(2))
            old = [src[3 + c, p] for c in range(3)]
            hx, hy, hz = (v * stay for v in old)
            hx = hx - 0.5 * ((y_up(ez) - ez) - (uy - ey))
            hy = hy - 0.5 * ((ux - ex) - (x_up(ez) - ez))
            hz = hz - 0.5 * ((x_up(ey) - ey) - (y_up(ex) - ex))
            new = [jnp.where(h_rows, n, o) for n, o in zip((hx, hy, hz), old)]
            return raw, (ex, ey, ez), new

        def store_h(p, new):
            for c in range(3):
                dst[3 + c, p - off] = new[c]

        _, _, new = magnetic(k)
        if dst is src:
            store_h(k, new)

        def plane(p, below):
            raw, e, new = magnetic(p)
            store_h(p, new)
            hx, hy, hz = new
            slot = slot_of(p)
            under = jnp.where(slot == cut, 0.0, 1.0).astype(F32)
            bx, by = (v * under for v in below)
            cx = (hz - y_down(hz, 1, p)) - (hy - by)
            cy = (hx - bx) - (hz - x_down(hz))
            cz = (hy - x_down(hy)) - (hx - y_down(hx, 0, p))
            entered = jnp.full(tile, slot, jnp.int32) < cut
            eps, half_sigma, kerr = (
                jnp.where(entered, coef_inc[i, p], coef[i, p]) for i in range(3)
            )
            permit = eps + kerr * (e[0] * e[0] + e[1] * e[1] + e[2] * e[2])
            inverse = 1.0 / (permit + half_sigma)
            scale = (permit - half_sigma) * inverse
            half_inverse = 0.5 * inverse
            for c, curl in enumerate((cx, cy, cz)):
                updated = scale * e[c] + half_inverse * curl
                dst[c, p - off] = jnp.where(e_rows, updated, raw[c])
            return hx, hy

        lax.fori_loop(k + 1, ext - 1 - k, plane, (new[0], new[1]), unroll=2)

    for k in range(HALF):
        level(k, k, fa, fa, 0, ca, cia, False, False, False)

    def pack_up(p, carry):
        for c in range(3):
            sb1[c, p] = jnp.where(low_rows, half_turn(fa[c, p]), fa[3 + c, p])
        return carry

    lax.fori_loop(0, ext, pack_up, 0)
    for i in range(pz // 4):
        packed = jnp.zeros(tile, F32)
        for j in range(4):
            for n, c in enumerate((0, 2)):
                at = 2 * j + n
                moved = pltpu.roll(fa[3 + c, HALF + 4 * i + j], (at + 8 - (HALF - 1)) % 8, 0)
                packed = jnp.where(row == at, moved, packed)
        xb[i] = packed
    up = [remote(sb1, rb1, 8, ydev(1)), remote(xb, rx, 9, ydev(1))]
    for copy in up:
        copy.start()

    inc_copy.wait()
    mat_copy.wait()

    def joined(low, own):
        return jnp.where(low_rows, low, half_turn(own))

    def shifted_coefs(i, carry):
        pair = rm[i]
        put(cb, 2 * i, lookup(joined(pair, ma[2 * i])))
        put(cb, 2 * i + 1, lookup(joined(half_turn(pair), ma[2 * i + 1])))
        entry = inc_plane(2 * i)
        pair = ri[entry // 2]
        put(cib, 2 * i, lookup(joined(pair, inc[entry])))
        put(cib, 2 * i + 1, lookup(joined(half_turn(pair), inc[entry + 1])))
        return carry

    lax.fori_loop(0, ext // 2, shifted_coefs, 0)
    for copy in up:
        copy.wait()

    def join_up(p, carry):
        for c in range(3):
            got = rb1[c, p]
            fb[c, p] = jnp.where(low_rows, got, half_turn(fa[c, p]))
            fb[3 + c, p] = half_turn(jnp.where(low_rows, fa[3 + c, p], got))
        return carry

    lax.fori_loop(0, ext, join_up, 0)
    for i in range(pz // 4):
        got = rx[i]
        for j in range(4):
            for n in range(2):
                at = 2 * j + n
                face[n, 4 * i + j] = got if at == 0 else pltpu.roll(got, 8 - at, 0)

    for k in range(HALF):
        level(k, k, fb, fb if k < HALF - 1 else fc, 0, cb, cib, True, True, k == HALF - 1)

    edges = [
        remote(fc.at[:, pl.ds(pz, HALF)], fc.at[:, lo_halo], 10, zdev(1)),
        remote(fc.at[:, pl.ds(HALF, HALF)], fc.at[:, hi_halo], 11, zdev(-1)),
    ]
    for copy in edges:
        copy.start()
    for copy in edges:
        copy.wait()

    for k in range(HALF):
        level(HALF + k, k, fc, fc, 0, cb, cib, False, True, False)

    def pack_down(p, carry):
        for c in range(3):
            sb2[c, p] = jnp.where(low_rows, fc[c, p], half_turn(fc[3 + c, p]))
        return carry

    lax.fori_loop(0, ext, pack_down, 0)
    down = remote(sb2, rb2, 12, ydev(-1))
    down.start()
    for n, c in enumerate((0, 2)):
        for p in range(pz):
            face[n, p] = pltpu.roll(fc[3 + c, HALF + p], 8 - (HALF - 1), 0) * face_ok
    down.wait()

    def join_down(p, carry):
        for c in range(3):
            got = rb2[c, p]
            fb[c, p] = half_turn(jnp.where(low_rows, got, fc[c, p]))
            fb[3 + c, p] = jnp.where(low_rows, half_turn(fc[3 + c, p]), got)
        return carry

    lax.fori_loop(0, ext, join_down, 0)

    for k in range(HALF):
        last = k == HALF - 1
        level(HALF + k, k, fb, fo if last else fb, HALF if last else 0, ca, cia, True, False, last)

    result = [
        remote(fo.at[pl.ds(0, 3)], o_e, 13, zdev(-2)),
        remote(fo.at[pl.ds(3, 3)], o_h, 14, zdev(-2)),
    ]
    for copy in result:
        copy.start()
    for copy in result:
        copy.wait()


def body(electric, magnetic, material, incoming, shift_flags, eps_table, sigma_table, kerr_table):
    _, pz, py, nx = electric.shape
    ext = pz + 2 * HALF
    n_inc = incoming.shape[0]
    vmem = pl.BlockSpec(memory_space=pltpu.VMEM)
    smem = pl.BlockSpec(memory_space=pltpu.SMEM)

    def buf(*dims, dtype=F32):
        return pltpu.VMEM((*dims, py, nx), dtype)

    ids = jnp.int32
    return pl.pallas_call(
        kernel,
        out_shape=(
            jax.ShapeDtypeStruct(electric.shape, F32),
            jax.ShapeDtypeStruct(magnetic.shape, F32),
        ),
        in_specs=[smem] * 4 + [vmem] * 4,
        out_specs=(vmem, vmem),
        scratch_shapes=[
            buf(6, ext), buf(6, ext), buf(6, ext), buf(6, pz),
            buf(3, ext), buf(3, ext), buf(3, ext), buf(3, ext),
            buf(ext, dtype=ids), buf(2, pz),
            buf(ext // 2, dtype=ids), buf(ext // 2, dtype=ids),
            buf(n_inc // 2, dtype=ids), buf(n_inc // 2, dtype=ids),
            buf(3, ext), buf(3, ext),
            buf(pz // 4), buf(pz // 4),
            buf(3, ext), buf(3, ext),
            pltpu.SemaphoreType.DMA((15,)),
            pltpu.SemaphoreType.DMA((15,)),
        ],
        compiler_params=pltpu.CompilerParams(
            collective_id=0, has_side_effects=True, vmem_limit_bytes=48 * 1024 * 1024
        ),
        name="window_steps",
    )(shift_flags, eps_table, sigma_table, kerr_table, electric, magnetic, material, incoming)


def solution(mesh):
    return jax.shard_map(
        body,
        mesh=mesh,
        in_specs=(
            P(None, "gz", "gy", None),
            P(None, "gz", "gy", None),
            P("gz", "gy", None),
            P(None, "gy", None),
            P(),
            P(),
            P(),
            P(),
        ),
        out_specs=(P(None, "gz", "gy", None), P(None, "gz", "gy", None)),
        check_vma=False,
    )
```

```python
import jax
import jax.numpy as jnp
from jax import lax
from jax.experimental import pallas as pl
from jax.experimental.pallas import tpu as pltpu
from jax.sharding import PartitionSpec as P

STEPS = 8
SHIFT = 8
HALF = 4
MESH = pl.DeviceIdType.MESH
F32 = jnp.float32


def kernel(
    flags, eps_t, sig_t, ker_t, e_in, h_in, mat, inc,
    o_e, o_h,
    fa, fb, fc, fo, ca, cia, cb, cib, ma, face, zs_lo, zs_hi,
    sm, rm, si, ri, sb1, rb1, sb2, rb2, ss, rs,
):
    nz_dev = lax.axis_size("gz")
    ny_dev = lax.axis_size("gy")
    g = lax.axis_index("gz")
    y = lax.axis_index("gy")
    pz = e_in.shape[1]
    nx = e_in.shape[3]
    slots = nz_dev * pz
    ext = pz + 2 * HALF
    tile = (8, nx)
    parts = pz // HALF

    def zdev(d):
        return (lax.rem(g + d + nz_dev, nz_dev), y)

    def ydev(d):
        return (g, lax.rem(y + d + ny_dev, ny_dev))

    barrier = pltpu.get_barrier_semaphore()
    partners = [zdev(1), zdev(-1), ydev(1), ydev(-1), zdev(2), zdev(-2)]
    for dev in partners:
        pl.semaphore_signal(barrier, inc=1, device_id=dev, device_id_type=MESH)

    row = lax.broadcasted_iota(jnp.int32, tile, 0)
    lane = lax.broadcasted_iota(jnp.int32, tile, 1)
    low_rows = row < HALF
    first_lane = lane == 0
    last_lane = lane == nx - 1
    at_edge = y == 0
    up_cut = jnp.where((row == HALF - 1) & at_edge, 0.0, 1.0).astype(F32)
    down_cut = jnp.where((row == HALF) & at_edge, 0.0, 1.0).astype(F32)
    face_ok = jnp.where(at_edge, 0.0, 1.0).astype(F32)

    def half_turn(v):
        return pltpu.roll(v, HALF, 0)

    sem_count = [0]

    def remote(src, dst, dev):
        n = sem_count[0]
        sem_count[0] += 1
        return pltpu.make_async_remote_copy(
            src, dst, ss.at[n], rs.at[n], device_id=dev, device_id_type=MESH
        )

    started = []

    def start(*copies):
        for copy in copies:
            copy.start()
            started.append(copy)

    def loop(lo, hi, step_fn, carry=0, most=6):
        n = hi - lo
        unroll = max(d for d in range(1, most + 1) if n % d == 0)
        return lax.fori_loop(lo, hi, step_fn, carry, unroll=unroll)

    def pack_ids(dst, src, i, j):
        dst[i] = jnp.where(low_rows, half_turn(src[j]), src[j + 1])

    for i in range(pz // 2):
        pack_ids(sm, mat, HALF // 2 + i, 2 * i)
    for i in range(inc.shape[0] // 2):
        pack_ids(si, inc, i, 2 * i)

    pl.semaphore_wait(barrier, len(partners))

    top = pl.ds(pz - HALF, HALF)
    bottom = pl.ds(0, HALF)
    lo_halo = pl.ds(0, HALF)
    hi_halo = pl.ds(HALF + pz, HALF)
    first_lo = [
        remote(e_in.at[:, top], fa.at[pl.ds(0, 3), lo_halo], zdev(1)),
        remote(h_in.at[:, top], fa.at[pl.ds(3, 3), lo_halo], zdev(1)),
        remote(mat.at[top], ma.at[lo_halo], zdev(1)),
    ]
    first_hi = [
        remote(e_in.at[:, bottom], fa.at[pl.ds(0, 3), hi_halo], zdev(-1)),
        remote(h_in.at[:, bottom], fa.at[pl.ds(3, 3), hi_halo], zdev(-1)),
        remote(mat.at[bottom], ma.at[hi_halo], zdev(-1)),
    ]
    start(*first_lo, *first_hi)
    half_ids = HALF // 2
    own_ids = pl.ds(half_ids, pz // 2)
    ids_up = [remote(sm.at[own_ids], rm.at[own_ids], ydev(1)), remote(si, ri, ydev(1))]
    start(*ids_up)

    for c in range(3):
        fa[c, HALF : HALF + pz] = e_in[c]
        fa[3 + c, HALF : HALF + pz] = h_in[c]
    ma[HALF : HALF + pz] = mat[...]

    def lookup(ids):
        out = [jnp.zeros(tile, F32) for _ in range(3)]
        for t in range(eps_t.shape[0]):
            here = ids == t
            for i, tab in enumerate((eps_t, sig_t, ker_t)):
                out[i] = jnp.where(here, tab[t], out[i])
        return out[0], 0.5 * out[1], out[2]

    def slot_of(p):
        return lax.rem(g * pz - HALF + p + slots, slots)

    def put(ref, p, values):
        for i in range(3):
            ref[i, p] = values[i]

    def inc_plane(p):
        return lax.rem(slot_of(p), inc.shape[0])

    def own_incoming(p, carry):
        put(cia, p, lookup(inc[inc_plane(p)]))
        return carry

    def own_material(p, carry):
        put(ca, p, lookup(ma[p]))
        return carry

    loop(HALF, HALF + pz, own_material, most=4)
    loop(0, ext, own_incoming, most=4)

    for copy in first_lo + first_hi:
        copy.wait_recv()
    for i in (0, 1, ext // 2 - 2, ext // 2 - 1):
        pack_ids(sm, ma, i, 2 * i)
    for at in (0, ext // 2 - half_ids):
        ends = pl.ds(at, half_ids)
        ids_up.append(remote(sm.at[ends], rm.at[ends], ydev(1)))
    start(*ids_up[2:])
    loop(0, HALF, own_material, most=4)
    loop(HALF + pz, ext, own_material, most=4)

    counts = []
    total = jnp.int32(0)
    for s in range(STEPS):
        total = total + flags[s]
        counts.append(total)

    def x_up(v):
        return jnp.where(last_lane, 0.0, pltpu.roll(v, nx - 1, 1))

    def x_down(v):
        return jnp.where(first_lane, 0.0, pltpu.roll(v, 1, 1))

    class Level:
        def __init__(self, step, k, src, dst, off, coefs, inverted, shifted):
            self.k, self.src, self.dst, self.off = k, src, dst, off
            self.coef, self.coef_inc = coefs
            self.shifted = shifted
            self.use_face = inverted and k == HALF - 1
            if inverted:
                self.h_rows = (row >= HALF - 1 - k) & (row < HALF + k)
                self.e_rows = (row >= HALF - 1 - k) & (row < HALF + 1 + k)
            else:
                self.h_rows = (row >= k) & (row < 2 * HALF - 1 - k)
                self.e_rows = (row >= k + 1) & (row < 2 * HALF - 1 - k)
            self.flag = flags[step] == 1
            self.cut = counts[step] * SHIFT

        def keep(self, p):
            slot = slot_of(p)
            fresh = self.flag & (slot < self.cut) & (slot >= self.cut - SHIFT)
            return jnp.where(fresh, 0.0, 1.0).astype(F32)

        def y_up(self, v):
            v = pltpu.roll(v, 7, 0)
            return v * up_cut if self.shifted else v

        def y_down(self, v, face_no, p):
            v = pltpu.roll(v, 1, 0)
            if self.shifted:
                v = v * down_cut
            if self.use_face:
                v = jnp.where(row == 0, face[face_no, p - HALF], v)
            return v

        def raw_e(self, p):
            return [self.src[c, p] for c in range(3)]

        def magnetic(self, p, store):
            stay = self.keep(p)
            on_cut = slot_of(p) == lax.rem(self.cut + slots - 1, slots)
            above = jnp.where(on_cut, 0.0, 1.0).astype(F32) * self.keep(p + 1)
            ex, ey, ez = (v * stay for v in self.raw_e(p))
            ux, uy = (self.src[c, p + 1] * above for c in range(2))
            old = [self.src[3 + c, p] for c in range(3)]
            hx, hy, hz = (v * stay for v in old)
            hx = hx - 0.5 * ((self.y_up(ez) - ez) - (uy - ey))
            hy = hy - 0.5 * ((ux - ex) - (x_up(ez) - ez))
            hz = hz - 0.5 * ((x_up(ey) - ey) - (self.y_up(ex) - ex))
            new = [jnp.where(self.h_rows, n, o) for n, o in zip((hx, hy, hz), old)]
            if store:
                for c in range(3):
                    self.dst[3 + c, p - self.off] = new[c]
            return tuple(new)

        def electric(self, p, raw, here, below):
            slot = slot_of(p)
            stay = self.keep(p)
            ex, ey, ez = e = [v * stay for v in raw]
            under = jnp.where(slot == self.cut, 0.0, 1.0).astype(F32)
            hx, hy, hz = here
            bx, by = (v * under for v in below)
            cx = (hz - self.y_down(hz, 1, p)) - (hy - by)
            cy = (hx - bx) - (hz - x_down(hz))
            cz = (hy - x_down(hy)) - (hx - self.y_down(hx, 0, p))
            entered = jnp.full(tile, slot, jnp.int32) < self.cut
            eps, half_sigma, kerr = (
                jnp.where(entered, self.coef_inc[i, p], self.coef[i, p]) for i in range(3)
            )
            permit = eps + kerr * (ex * ex + ey * ey + ez * ez)
            inverse = 1.0 / (permit + half_sigma)
            scale = (permit - half_sigma) * inverse
            half_inverse = 0.5 * inverse
            for c, curl in enumerate((cx, cy, cz)):
                updated = scale * e[c] + half_inverse * curl
                self.dst[c, p - self.off] = jnp.where(self.e_rows, updated, raw[c])

        def upward(self, part):
            k = self.k
            lo = k + 1 if part == 0 else 2 * HALF + 3 + HALF * (part - 1) - k
            hi = 2 * HALF + 3 + HALF * part - k
            if part == 0:
                below = self.magnetic(k, self.dst is self.src)[:2]
            else:
                below = tuple(self.dst[3 + c, lo - 1 - self.off] for c in range(2))

            def plane(p, below):
                raw = self.raw_e(p)
                here = self.magnetic(p, True)
                self.electric(p, raw, here, below)
                return here[:2]

            loop(lo, hi, plane, below)

        def downward(self, part):
            k = self.k
            hi = ext - 2 - k if part == 0 else pz - HALF * part + k
            lo = pz - HALF * (part + 1) + k
            if part == 0:
                above = self.magnetic(hi, True)
            else:
                above = tuple(self.dst[3 + c, hi - self.off] for c in range(3))
            split = part == parts - 1 and self.dst is not self.src

            def plane(p, above, store):
                raw = self.raw_e(p + 1)
                here = self.magnetic(p, store)
                self.electric(p + 1, raw, above, here[:2])
                return here

            end = lo + 1 if split else lo
            above = loop(0, hi - end, lambda i, above: plane(hi - 1 - i, above, True), above)
            if split:
                plane(lo, above, False)

    bounds = [0] + [2 * HALF + HALF * j for j in range(parts - 1)] + [ext]
    up_chunks = [(bounds[j], bounds[j + 1]) for j in range(parts)]
    down_chunks = [(ext - hi, ext - lo) for lo, hi in up_chunks]

    up = []
    at = 0
    levels = [Level(k, k, fa, fa, 0, (ca, cia), False, False) for k in range(HALF)]
    for part, (lo, hi) in enumerate(up_chunks):
        for level in levels:
            level.upward(part)
        base = at

        def pack_up(p, carry):
            for c in range(3):
                sb1[base + 3 * (p - lo) + c] = jnp.where(low_rows, half_turn(fa[c, p]), fa[3 + c, p])
            return carry

        loop(lo, hi, pack_up)
        at += 3 * (hi - lo)
        packed = jnp.zeros(tile, F32)
        for j in range(HALF):
            for n, c in enumerate((0, 2)):
                to = 2 * j + n
                moved = pltpu.roll(fa[3 + c, HALF * (part + 1) + j], (to + 8 - (HALF - 1)) % 8, 0)
                packed = jnp.where(row == to, moved, packed)
        sb1[at] = packed
        at += 1
        span = pl.ds(base, at - base)
        up.append(remote(sb1.at[span], rb1.at[span], ydev(1)))
        start(up[-1])

    for copy in ids_up:
        copy.wait_recv()

    def joined(low, own):
        return jnp.where(low_rows, low, half_turn(own))

    def shifted_coefs(i, carry):
        pair = rm[i]
        put(cb, 2 * i, lookup(joined(pair, ma[2 * i])))
        put(cb, 2 * i + 1, lookup(joined(half_turn(pair), ma[2 * i + 1])))
        entry = inc_plane(2 * i)
        pair = ri[entry // 2]
        put(cib, 2 * i, lookup(joined(pair, inc[entry])))
        put(cib, 2 * i + 1, lookup(joined(half_turn(pair), inc[entry + 1])))
        return carry

    loop(0, ext // 2, shifted_coefs, most=2)

    def join_up(part):
        lo, hi = up_chunks[part]
        base = 3 * lo + part
        up[part].wait_recv()

        def join(p, carry):
            for c in range(3):
                got = rb1[base + 3 * (p - lo) + c]
                fb[c, p] = jnp.where(low_rows, got, half_turn(fa[c, p]))
                fb[3 + c, p] = half_turn(jnp.where(low_rows, fa[3 + c, p], got))
            return carry

        loop(lo, hi, join)
        got = rb1[base + 3 * (hi - lo)]
        for j in range(HALF):
            for n in range(2):
                frm = 2 * j + n
                face[n, HALF * part + j] = got if frm == 0 else pltpu.roll(got, 8 - frm, 0)

    levels = [
        Level(k, k, fb, fb if k < HALF - 1 else fc, 0, (cb, cib), True, True) for k in range(HALF)
    ]
    join_up(0)
    for part in range(parts):
        if part < parts - 1:
            join_up(part + 1)
        for level in levels:
            level.upward(part)
        if part == 0:
            zs_lo[...] = fc[:, HALF : 2 * HALF]
            to_hi = remote(zs_lo, fc.at[:, hi_halo], zdev(-1))
            start(to_hi)
    zs_hi[...] = fc[:, pz : pz + HALF]
    to_lo = remote(zs_hi, fc.at[:, lo_halo], zdev(1))
    start(to_lo)
    to_hi.wait_recv()

    down = []
    levels = [Level(HALF + k, k, fc, fc, 0, (cb, cib), False, True) for k in range(HALF)]
    for part, (lo, hi) in enumerate(down_chunks):
        if part == parts - 1:
            to_lo.wait_recv()
        for level in levels:
            level.downward(part)

        def pack_down(p, carry):
            for c in range(3):
                sb2[3 * p + c] = jnp.where(low_rows, fc[c, p], half_turn(fc[3 + c, p]))
            return carry

        loop(lo, hi, pack_down)
        span = pl.ds(3 * lo, 3 * (hi - lo))
        down.append(remote(sb2.at[span], rb2.at[span], ydev(-1)))
        start(down[-1])

    for p in range(pz):
        for n, c in enumerate((0, 2)):
            face[n, p] = pltpu.roll(fc[3 + c, HALF + p], 8 - (HALF - 1), 0) * face_ok

    def join_down(part):
        lo, hi = down_chunks[part]
        down[part].wait_recv()

        def join(p, carry):
            for c in range(3):
                got = rb2[3 * p + c]
                fb[c, p] = half_turn(jnp.where(low_rows, got, fc[c, p]))
                fb[3 + c, p] = jnp.where(low_rows, half_turn(fc[3 + c, p]), got)
            return carry

        loop(lo, hi, join)

    levels = []
    for k in range(HALF):
        last = k == HALF - 1
        levels.append(Level(HALF + k, k, fb, fo if last else fb, HALF if last else 0, (ca, cia), True, False))
    results = []
    join_down(0)
    for part in range(parts):
        if part < parts - 1:
            join_down(part + 1)
        for level in levels:
            level.downward(part)
        done = pl.ds(pz - HALF * (part + 1), HALF)
        results += [
            remote(fo.at[pl.ds(0, 3), done], o_e.at[:, done], zdev(-2)),
            remote(fo.at[pl.ds(3, 3), done], o_h.at[:, done], zdev(-2)),
        ]
        start(*results[-2:])
    for copy in results:
        copy.wait_recv()
    for copy in started:
        copy.wait_send()


def body(electric, magnetic, material, incoming, shift_flags, eps_table, sigma_table, kerr_table):
    _, pz, py, nx = electric.shape
    ext = pz + 2 * HALF
    n_inc = incoming.shape[0]
    tiles = 3 * ext + pz // HALF
    vmem = pl.BlockSpec(memory_space=pltpu.VMEM)
    smem = pl.BlockSpec(memory_space=pltpu.SMEM)

    def buf(*dims, dtype=F32):
        return pltpu.VMEM((*dims, py, nx), dtype)

    ids = jnp.int32
    return pl.pallas_call(
        kernel,
        out_shape=(
            jax.ShapeDtypeStruct(electric.shape, F32),
            jax.ShapeDtypeStruct(magnetic.shape, F32),
        ),
        in_specs=[smem] * 4 + [vmem] * 4,
        out_specs=(vmem, vmem),
        scratch_shapes=[
            buf(6, ext), buf(6, ext), buf(6, ext), buf(6, pz),
            buf(3, ext), buf(3, ext), buf(3, ext), buf(3, ext),
            buf(ext, dtype=ids), buf(2, pz), buf(6, HALF), buf(6, HALF),
            buf(ext // 2, dtype=ids), buf(ext // 2, dtype=ids),
            buf(n_inc // 2, dtype=ids), buf(n_inc // 2, dtype=ids),
            buf(tiles), buf(tiles), buf(3 * ext), buf(3 * ext),
            pltpu.SemaphoreType.DMA((28,)),
            pltpu.SemaphoreType.DMA((28,)),
        ],
        compiler_params=pltpu.CompilerParams(
            collective_id=0, has_side_effects=True, vmem_limit_bytes=48 * 1024 * 1024
        ),
        name="window_steps",
    )(shift_flags, eps_table, sigma_table, kerr_table, electric, magnetic, material, incoming)


def solution(mesh):
    return jax.shard_map(
        body,
        mesh=mesh,
        in_specs=(
            P(None, "gz", "gy", None),
            P(None, "gz", "gy", None),
            P("gz", "gy", None),
            P(None, "gy", None),
            P(),
            P(),
            P(),
            P(),
        ),
        out_specs=(P(None, "gz", "gy", None), P(None, "gz", "gy", None)),
        check_vma=False,
    )
```

```python
import jax
import jax.numpy as jnp
from jax import lax
from jax.experimental import pallas as pl
from jax.experimental.pallas import tpu as pltpu
from jax.sharding import PartitionSpec as P

STEPS = 8
SHIFT = 8
HALF = 4
MESH = pl.DeviceIdType.MESH
F32 = jnp.float32


def kernel(
    flags_in, eps_in, sig_in, ker_in, e_in, h_in, mat_in, inc_in,
    o_e, o_h,
    flags, eps_t, sig_t, ker_t, inc, fa, fb, fc, fo, ca, cia, cb, cib, ma, face, zs_lo, zs_hi,
    sm, rm, si, ri, sb1, rb1, sb2, rb2, ss, rs, ls,
):
    nz_dev = lax.axis_size("gz")
    ny_dev = lax.axis_size("gy")
    g = lax.axis_index("gz")
    y = lax.axis_index("gy")
    pz = e_in.shape[1]
    nx = e_in.shape[3]
    slots = nz_dev * pz
    ext = pz + 2 * HALF
    tile = (8, nx)
    parts = pz // HALF

    def zdev(d):
        return (lax.rem(g + d + nz_dev, nz_dev), y)

    def ydev(d):
        return (g, lax.rem(y + d + ny_dev, ny_dev))

    barrier = pltpu.get_barrier_semaphore()
    partners = [zdev(1), zdev(-1), ydev(1), ydev(-1), zdev(2), zdev(-2)]
    for dev in partners:
        pl.semaphore_signal(barrier, inc=1, device_id=dev, device_id_type=MESH)

    row = lax.broadcasted_iota(jnp.int32, tile, 0)
    lane = lax.broadcasted_iota(jnp.int32, tile, 1)
    low_rows = row < HALF
    first_lane = lane == 0
    last_lane = lane == nx - 1
    at_edge = y == 0
    up_cut = jnp.where((row == HALF - 1) & at_edge, 0.0, 1.0).astype(F32)
    down_cut = jnp.where((row == HALF) & at_edge, 0.0, 1.0).astype(F32)
    face_ok = jnp.where(at_edge, 0.0, 1.0).astype(F32)

    def half_turn(v):
        return pltpu.roll(v, HALF, 0)

    sem_count = [0]

    def remote(src, dst, dev):
        n = sem_count[0]
        sem_count[0] += 1
        return pltpu.make_async_remote_copy(
            src, dst, ss.at[n], rs.at[n], device_id=dev, device_id_type=MESH
        )

    started = []

    def start(*copies):
        for copy in copies:
            copy.start()
            started.append(copy)

    def loop(lo, hi, step_fn, carry=0, most=6):
        n = hi - lo
        unroll = max(d for d in range(1, most + 1) if n % d == 0)
        return lax.fori_loop(lo, hi, step_fn, carry, unroll=unroll)

    def pack_ids(dst, src, i):
        dst[i] = jnp.where(low_rows, half_turn(src[2 * i]), src[2 * i + 1])

    top = pl.ds(pz - HALF, HALF)
    bottom = pl.ds(0, HALF)
    lo_halo = pl.ds(0, HALF)
    hi_halo = pl.ds(HALF + pz, HALF)
    own = pl.ds(HALF, pz)
    fields = [(e_in, 0), (h_in, 3)]
    inputs = [
        (inc_in, inc),
        (mat_in, ma.at[own]),
        (flags_in, flags),
        (eps_in, eps_t),
        (sig_in, sig_t),
        (ker_in, ker_t),
    ] + [(ref, fa.at[pl.ds(c, 3), own]) for ref, c in fields]
    inputs = [pltpu.make_async_copy(src, dst, ls.at[i]) for i, (src, dst) in enumerate(inputs)]
    for copy in inputs:
        copy.start()

    first_lo = [remote(mat_in.at[top], ma.at[lo_halo], zdev(1))] + [
        remote(ref.at[:, top], fa.at[pl.ds(c, 3), lo_halo], zdev(1)) for ref, c in fields
    ]
    first_hi = [remote(mat_in.at[bottom], ma.at[hi_halo], zdev(-1))] + [
        remote(ref.at[:, bottom], fa.at[pl.ds(c, 3), hi_halo], zdev(-1)) for ref, c in fields
    ]

    pl.semaphore_wait(barrier, len(partners))
    start(*first_lo, *first_hi)

    for copy in inputs:
        copy.wait()
    half_ids = HALF // 2
    own_ids = pl.ds(half_ids, pz // 2)
    for i in range(pz // 2):
        pack_ids(sm, ma, half_ids + i)
    for i in range(inc.shape[0] // 2):
        pack_ids(si, inc, i)
    ids_up = [remote(sm.at[own_ids], rm.at[own_ids], ydev(1)), remote(si, ri, ydev(1))]
    start(*ids_up)

    def lookup(ids):
        out = [jnp.zeros(tile, F32) for _ in range(3)]
        for t in range(eps_t.shape[0]):
            here = ids == t
            for i, tab in enumerate((eps_t, sig_t, ker_t)):
                out[i] = jnp.where(here, tab[t], out[i])
        return out[0], 0.5 * out[1], out[2]

    def slot_of(p):
        return lax.rem(g * pz - HALF + p + slots, slots)

    def put(ref, p, values):
        for i in range(3):
            ref[i, p] = values[i]

    def inc_plane(p):
        return lax.rem(slot_of(p), inc.shape[0])

    def own_incoming(p, carry):
        put(cia, p, lookup(inc[inc_plane(p)]))
        return carry

    def own_material(p, carry):
        put(ca, p, lookup(ma[p]))
        return carry

    loop(HALF, HALF + pz, own_material, most=4)
    loop(0, ext, own_incoming, most=4)

    for copy in first_lo + first_hi[:1]:
        copy.wait_recv()
    for at in (0, ext // 2 - half_ids):
        for i in range(half_ids):
            pack_ids(sm, ma, at + i)
        ends = pl.ds(at, half_ids)
        ids_up.append(remote(sm.at[ends], rm.at[ends], ydev(1)))
    start(*ids_up[2:])
    loop(0, HALF, own_material, most=4)
    loop(HALF + pz, ext, own_material, most=4)

    counts = []
    total = jnp.int32(0)
    for s in range(STEPS):
        total = total + flags[s]
        counts.append(total)

    def x_up(v):
        return jnp.where(last_lane, 0.0, pltpu.roll(v, nx - 1, 1))

    def x_down(v):
        return jnp.where(first_lane, 0.0, pltpu.roll(v, 1, 1))

    class Level:
        def __init__(self, step, k, src, dst, off, coefs, inverted, shifted):
            self.k, self.src, self.dst, self.off = k, src, dst, off
            self.coef, self.coef_inc = coefs
            self.shifted = shifted
            self.use_face = inverted and k == HALF - 1
            if inverted:
                self.h_rows = (row >= HALF - 1 - k) & (row < HALF + k)
                self.e_rows = (row >= HALF - 1 - k) & (row < HALF + 1 + k)
            else:
                self.h_rows = (row >= k) & (row < 2 * HALF - 1 - k)
                self.e_rows = (row >= k + 1) & (row < 2 * HALF - 1 - k)
            self.flag = flags[step] == 1
            self.cut = counts[step] * SHIFT

        def keep(self, p):
            slot = slot_of(p)
            fresh = self.flag & (slot < self.cut) & (slot >= self.cut - SHIFT)
            return jnp.where(fresh, 0.0, 1.0).astype(F32)

        def y_up(self, v):
            v = pltpu.roll(v, 7, 0)
            return v * up_cut if self.shifted else v

        def y_down(self, v, face_no, p):
            v = pltpu.roll(v, 1, 0)
            if self.shifted:
                v = v * down_cut
            if self.use_face:
                v = jnp.where(row == 0, face[face_no, p - HALF], v)
            return v

        def raw_e(self, p):
            return [self.src[c, p] for c in range(3)]

        def magnetic(self, p, store):
            stay = self.keep(p)
            on_cut = slot_of(p) == lax.rem(self.cut + slots - 1, slots)
            above = jnp.where(on_cut, 0.0, 1.0).astype(F32) * self.keep(p + 1)
            ex, ey, ez = (v * stay for v in self.raw_e(p))
            ux, uy = (self.src[c, p + 1] * above for c in range(2))
            old = [self.src[3 + c, p] for c in range(3)]
            hx, hy, hz = (v * stay for v in old)
            hx = hx - 0.5 * ((self.y_up(ez) - ez) - (uy - ey))
            hy = hy - 0.5 * ((ux - ex) - (x_up(ez) - ez))
            hz = hz - 0.5 * ((x_up(ey) - ey) - (self.y_up(ex) - ex))
            new = [jnp.where(self.h_rows, n, o) for n, o in zip((hx, hy, hz), old)]
            if store:
                for c in range(3):
                    self.dst[3 + c, p - self.off] = new[c]
            return tuple(new)

        def electric(self, p, raw, here, below):
            slot = slot_of(p)
            stay = self.keep(p)
            ex, ey, ez = e = [v * stay for v in raw]
            under = jnp.where(slot == self.cut, 0.0, 1.0).astype(F32)
            hx, hy, hz = here
            bx, by = (v * under for v in below)
            cx = (hz - self.y_down(hz, 1, p)) - (hy - by)
            cy = (hx - bx) - (hz - x_down(hz))
            cz = (hy - x_down(hy)) - (hx - self.y_down(hx, 0, p))
            entered = jnp.full(tile, slot, jnp.int32) < self.cut
            eps, half_sigma, kerr = (
                jnp.where(entered, self.coef_inc[i, p], self.coef[i, p]) for i in range(3)
            )
            permit = eps + kerr * (ex * ex + ey * ey + ez * ez)
            inverse = 1.0 / (permit + half_sigma)
            scale = (permit - half_sigma) * inverse
            half_inverse = 0.5 * inverse
            for c, curl in enumerate((cx, cy, cz)):
                updated = scale * e[c] + half_inverse * curl
                self.dst[c, p - self.off] = jnp.where(self.e_rows, updated, raw[c])

        def upward(self, part):
            k = self.k
            lo = k + 1 if part == 0 else 2 * HALF + 3 + HALF * (part - 1) - k
            hi = 2 * HALF + 3 + HALF * part - k
            if part == 0:
                below = self.magnetic(k, self.dst is self.src)[:2]
            else:
                below = tuple(self.dst[3 + c, lo - 1 - self.off] for c in range(2))

            def plane(p, below):
                raw = self.raw_e(p)
                here = self.magnetic(p, True)
                self.electric(p, raw, here, below)
                return here[:2]

            loop(lo, hi, plane, below)

        def downward(self, part):
            k = self.k
            hi = ext - 2 - k if part == 0 else pz - HALF * part + k
            lo = pz - HALF * (part + 1) + k
            if part == 0:
                above = self.magnetic(hi, True)
            else:
                above = tuple(self.dst[3 + c, hi - self.off] for c in range(3))
            split = part == parts - 1 and self.dst is not self.src

            def plane(p, above, store):
                raw = self.raw_e(p + 1)
                here = self.magnetic(p, store)
                self.electric(p + 1, raw, above, here[:2])
                return here

            end = lo + 1 if split else lo
            above = loop(0, hi - end, lambda i, above: plane(hi - 1 - i, above, True), above)
            if split:
                plane(lo, above, False)

    bounds = [0] + [2 * HALF + HALF * j for j in range(parts - 1)] + [ext]
    up_chunks = [(bounds[j], bounds[j + 1]) for j in range(parts)]
    down_chunks = [(ext - hi, ext - lo) for lo, hi in up_chunks]

    up = []
    at = 0
    levels = [Level(k, k, fa, fa, 0, (ca, cia), False, False) for k in range(HALF)]
    for part, (lo, hi) in enumerate(up_chunks):
        if part == parts - 1:
            for copy in first_hi[1:]:
                copy.wait_recv()
        for level in levels:
            level.upward(part)
        base = at

        def pack_up(p, carry):
            for c in range(3):
                sb1[base + 3 * (p - lo) + c] = jnp.where(low_rows, half_turn(fa[c, p]), fa[3 + c, p])
            return carry

        loop(lo, hi, pack_up)
        at += 3 * (hi - lo)
        packed = jnp.zeros(tile, F32)
        for j in range(HALF):
            for n, c in enumerate((0, 2)):
                to = 2 * j + n
                moved = pltpu.roll(fa[3 + c, HALF * (part + 1) + j], (to + 8 - (HALF - 1)) % 8, 0)
                packed = jnp.where(row == to, moved, packed)
        sb1[at] = packed
        at += 1
        span = pl.ds(base, at - base)
        up.append(remote(sb1.at[span], rb1.at[span], ydev(1)))
        start(up[-1])

    for copy in ids_up:
        copy.wait_recv()

    def joined(low, own):
        return jnp.where(low_rows, low, half_turn(own))

    def shifted_coefs(i, carry):
        pair = rm[i]
        put(cb, 2 * i, lookup(joined(pair, ma[2 * i])))
        put(cb, 2 * i + 1, lookup(joined(half_turn(pair), ma[2 * i + 1])))
        entry = inc_plane(2 * i)
        pair = ri[entry // 2]
        put(cib, 2 * i, lookup(joined(pair, inc[entry])))
        put(cib, 2 * i + 1, lookup(joined(half_turn(pair), inc[entry + 1])))
        return carry

    loop(0, ext // 2, shifted_coefs, most=2)

    def join_up(part):
        lo, hi = up_chunks[part]
        base = 3 * lo + part
        up[part].wait_recv()

        def join(p, carry):
            for c in range(3):
                got = rb1[base + 3 * (p - lo) + c]
                fb[c, p] = jnp.where(low_rows, got, half_turn(fa[c, p]))
                fb[3 + c, p] = half_turn(jnp.where(low_rows, fa[3 + c, p], got))
            return carry

        loop(lo, hi, join)
        got = rb1[base + 3 * (hi - lo)]
        for j in range(HALF):
            for n in range(2):
                frm = 2 * j + n
                face[n, HALF * part + j] = got if frm == 0 else pltpu.roll(got, 8 - frm, 0)

    levels = [
        Level(k, k, fb, fb if k < HALF - 1 else fc, 0, (cb, cib), True, True) for k in range(HALF)
    ]
    join_up(0)
    for part in range(parts):
        if part < parts - 1:
            join_up(part + 1)
        for level in levels:
            level.upward(part)
        if part == 0:
            zs_lo[...] = fc[:, HALF : 2 * HALF]
            to_hi = remote(zs_lo, fc.at[:, hi_halo], zdev(-1))
            start(to_hi)
    zs_hi[...] = fc[:, pz : pz + HALF]
    to_lo = remote(zs_hi, fc.at[:, lo_halo], zdev(1))
    start(to_lo)
    to_hi.wait_recv()

    down = []
    levels = [Level(HALF + k, k, fc, fc, 0, (cb, cib), False, True) for k in range(HALF)]
    for part, (lo, hi) in enumerate(down_chunks):
        if part == parts - 1:
            to_lo.wait_recv()
        for level in levels:
            level.downward(part)

        def pack_down(p, carry):
            for c in range(3):
                sb2[3 * p + c] = jnp.where(low_rows, fc[c, p], half_turn(fc[3 + c, p]))
            return carry

        loop(lo, hi, pack_down)
        span = pl.ds(3 * lo, 3 * (hi - lo))
        down.append(remote(sb2.at[span], rb2.at[span], ydev(-1)))
        start(down[-1])

    for p in range(pz):
        for n, c in enumerate((0, 2)):
            face[n, p] = pltpu.roll(fc[3 + c, HALF + p], 8 - (HALF - 1), 0) * face_ok

    def join_down(part):
        lo, hi = down_chunks[part]
        down[part].wait_recv()

        def join(p, carry):
            for c in range(3):
                got = rb2[3 * p + c]
                fb[c, p] = half_turn(jnp.where(low_rows, got, fc[c, p]))
                fb[3 + c, p] = jnp.where(low_rows, half_turn(fc[3 + c, p]), got)
            return carry

        loop(lo, hi, join)

    levels = []
    for k in range(HALF):
        last = k == HALF - 1
        levels.append(Level(HALF + k, k, fb, fo if last else fb, HALF if last else 0, (ca, cia), True, False))
    crossing = lax.rem(g, nz_dev // 2) < 2
    results = []

    def start_results(copies, now):
        @pl.when(now)
        def _():
            for copy in copies:
                copy.start()

    join_down(0)
    for part in range(parts):
        if part < parts - 1:
            join_down(part + 1)
        for level in levels:
            level.downward(part)
        done = pl.ds(pz - HALF * (part + 1), HALF)
        results += [
            remote(fo.at[pl.ds(0, 3), done], o_e.at[:, done], zdev(-2)),
            remote(fo.at[pl.ds(3, 3), done], o_h.at[:, done], zdev(-2)),
        ]
        start_results(results[-2:], jnp.logical_not(crossing))
    start_results(results, crossing)
    for copy in results:
        copy.wait_recv()
    for copy in started + results:
        copy.wait_send()


def body(electric, magnetic, material, incoming, shift_flags, eps_table, sigma_table, kerr_table):
    _, pz, py, nx = electric.shape
    ext = pz + 2 * HALF
    n_inc = incoming.shape[0]
    tiles = 3 * ext + pz // HALF
    vmem = pl.BlockSpec(memory_space=pltpu.VMEM)

    def buf(*dims, dtype=F32):
        return pltpu.VMEM((*dims, py, nx), dtype)

    ids = jnp.int32
    return pl.pallas_call(
        kernel,
        out_shape=(
            jax.ShapeDtypeStruct(electric.shape, F32),
            jax.ShapeDtypeStruct(magnetic.shape, F32),
        ),
        in_specs=[pl.BlockSpec(memory_space=pltpu.HBM)] * 8,
        out_specs=(vmem, vmem),
        scratch_shapes=[
            pltpu.SMEM(shift_flags.shape, ids),
            *[pltpu.SMEM(t.shape, F32) for t in (eps_table, sigma_table, kerr_table)],
            buf(n_inc, dtype=ids),
            buf(6, ext), buf(6, ext), buf(6, ext), buf(6, pz),
            buf(3, ext), buf(3, ext), buf(3, ext), buf(3, ext),
            buf(ext, dtype=ids), buf(2, pz), buf(6, HALF), buf(6, HALF),
            buf(ext // 2, dtype=ids), buf(ext // 2, dtype=ids),
            buf(n_inc // 2, dtype=ids), buf(n_inc // 2, dtype=ids),
            buf(tiles), buf(tiles), buf(3 * ext), buf(3 * ext),
            pltpu.SemaphoreType.DMA((30,)),
            pltpu.SemaphoreType.DMA((30,)),
            pltpu.SemaphoreType.DMA((8,)),
        ],
        compiler_params=pltpu.CompilerParams(
            collective_id=0, has_side_effects=True, vmem_limit_bytes=67_000_000
        ),
        name="window_steps",
    )(shift_flags, eps_table, sigma_table, kerr_table, electric, magnetic, material, incoming)


def solution(mesh):
    return jax.shard_map(
        body,
        mesh=mesh,
        in_specs=(
            P(None, "gz", "gy", None),
            P(None, "gz", "gy", None),
            P("gz", "gy", None),
            P(None, "gy", None),
            P(),
            P(),
            P(),
            P(),
        ),
        out_specs=(P(None, "gz", "gy", None), P(None, "gz", "gy", None)),
        check_vma=False,
    )
```

```python
import jax
import jax.numpy as jnp
from jax import lax
from jax.experimental import pallas as pl
from jax.experimental.pallas import tpu as pltpu
from jax.sharding import PartitionSpec as P

STEPS = 8
SHIFT = 8
HALF = 4
MESH = pl.DeviceIdType.MESH
F32 = jnp.float32


def kernel(
    flags_in, eps_in, sig_in, ker_in, e_in, h_in, mat_in, inc_in,
    out,
    flags, eps_t, sig_t, ker_t, inc, fa, fb, fc, fo, ca, cia, cb, cib, ma, face, zs_lo, zs_hi,
    sm, rm, si, ri, sb1, rb1, sb2, rb2, ss, rs, ls,
):
    nz_dev = lax.axis_size("gz")
    ny_dev = lax.axis_size("gy")
    g = lax.axis_index("gz")
    y = lax.axis_index("gy")
    pz = e_in.shape[1]
    nx = e_in.shape[3]
    slots = nz_dev * pz
    ext = pz + 2 * HALF
    tile = (8, nx)
    parts = pz // HALF

    def zdev(d):
        return (lax.rem(g + d + nz_dev, nz_dev), y)

    def ydev(d):
        return (g, lax.rem(y + d + ny_dev, ny_dev))

    barrier = pltpu.get_barrier_semaphore()
    partners = [zdev(1), zdev(-1), ydev(1), ydev(-1), zdev(2), zdev(-2)]
    for dev in partners:
        pl.semaphore_signal(barrier, inc=1, device_id=dev, device_id_type=MESH)

    row = lax.broadcasted_iota(jnp.int32, tile, 0)
    lane = lax.broadcasted_iota(jnp.int32, tile, 1)
    low_rows = row < HALF
    first_lane = lane == 0
    last_lane = lane == nx - 1
    at_edge = y == 0
    up_cut = jnp.where((row == HALF - 1) & at_edge, 0.0, 1.0).astype(F32)
    down_cut = jnp.where((row == HALF) & at_edge, 0.0, 1.0).astype(F32)
    face_ok = jnp.where(at_edge, 0.0, 1.0).astype(F32)

    def half_turn(v):
        return pltpu.roll(v, HALF, 0)

    sem_count = [0]

    def remote(src, dst, dev):
        n = sem_count[0]
        sem_count[0] += 1
        return pltpu.make_async_remote_copy(
            src, dst, ss.at[n], rs.at[n], device_id=dev, device_id_type=MESH
        )

    started = []

    def start(*copies):
        for copy in copies:
            copy.start()
            started.append(copy)

    def loop(lo, hi, step_fn, carry=0, most=6):
        n = hi - lo
        unroll = max(d for d in range(1, most + 1) if n % d == 0)
        return lax.fori_loop(lo, hi, step_fn, carry, unroll=unroll)

    def pack_ids(dst, src, i):
        dst[i] = jnp.where(low_rows, half_turn(src[2 * i]), src[2 * i + 1])

    top = pl.ds(pz - HALF, HALF)
    bottom = pl.ds(0, HALF)
    lo_halo = pl.ds(0, HALF)
    hi_halo = pl.ds(HALF + pz, HALF)
    own = pl.ds(HALF, pz)
    fields = [(e_in, 0), (h_in, 3)]
    inputs = [
        (inc_in, inc),
        (mat_in, ma.at[own]),
        (flags_in, flags),
        (eps_in, eps_t),
        (sig_in, sig_t),
        (ker_in, ker_t),
    ] + [(ref, fa.at[pl.ds(c, 3), own]) for ref, c in fields]
    inputs = [pltpu.make_async_copy(src, dst, ls.at[i]) for i, (src, dst) in enumerate(inputs)]
    for copy in inputs:
        copy.start()

    first_lo = [remote(mat_in.at[top], ma.at[lo_halo], zdev(1))] + [
        remote(ref.at[:, top], fa.at[pl.ds(c, 3), lo_halo], zdev(1)) for ref, c in fields
    ]
    first_hi = [remote(mat_in.at[bottom], ma.at[hi_halo], zdev(-1))] + [
        remote(ref.at[:, bottom], fa.at[pl.ds(c, 3), hi_halo], zdev(-1)) for ref, c in fields
    ]

    pl.semaphore_wait(barrier, len(partners))
    start(*first_lo, *first_hi)

    for copy in inputs:
        copy.wait()
    half_ids = HALF // 2
    own_ids = pl.ds(half_ids, pz // 2)
    for i in range(pz // 2):
        pack_ids(sm, ma, half_ids + i)
    for i in range(inc.shape[0] // 2):
        pack_ids(si, inc, i)
    ids_up = [remote(sm.at[own_ids], rm.at[own_ids], ydev(1)), remote(si, ri, ydev(1))]
    start(*ids_up)

    def lookup(ids):
        out = [jnp.zeros(tile, F32) for _ in range(3)]
        for t in range(eps_t.shape[0]):
            here = ids == t
            for i, tab in enumerate((eps_t, sig_t, ker_t)):
                out[i] = jnp.where(here, tab[t], out[i])
        return out[0], 0.5 * out[1], out[2]

    def slot_of(p):
        return lax.rem(g * pz - HALF + p + slots, slots)

    def put(ref, p, values):
        for i in range(3):
            ref[i, p] = values[i]

    def inc_plane(p):
        return lax.rem(slot_of(p), inc.shape[0])

    def own_incoming(p, carry):
        put(cia, p, lookup(inc[inc_plane(p)]))
        return carry

    def own_material(p, carry):
        put(ca, p, lookup(ma[p]))
        return carry

    loop(HALF, HALF + pz, own_material, most=4)
    loop(0, ext, own_incoming, most=4)

    for copy in first_lo + first_hi[:1]:
        copy.wait_recv()
    for at in (0, ext // 2 - half_ids):
        for i in range(half_ids):
            pack_ids(sm, ma, at + i)
        ends = pl.ds(at, half_ids)
        ids_up.append(remote(sm.at[ends], rm.at[ends], ydev(1)))
    start(*ids_up[2:])
    loop(0, HALF, own_material, most=4)
    loop(HALF + pz, ext, own_material, most=4)

    counts = []
    total = jnp.int32(0)
    for s in range(STEPS):
        total = total + flags[s]
        counts.append(total)

    def x_up(v):
        return jnp.where(last_lane, 0.0, pltpu.roll(v, nx - 1, 1))

    def x_down(v):
        return jnp.where(first_lane, 0.0, pltpu.roll(v, 1, 1))

    class Level:
        def __init__(self, step, k, src, dst, off, coefs, inverted, shifted):
            self.k, self.src, self.dst, self.off = k, src, dst, off
            self.coef, self.coef_inc = coefs
            self.shifted = shifted
            self.use_face = inverted and k == HALF - 1
            if inverted:
                self.h_rows = (row >= HALF - 1 - k) & (row < HALF + k)
                self.e_rows = (row >= HALF - 1 - k) & (row < HALF + 1 + k)
            else:
                self.h_rows = (row >= k) & (row < 2 * HALF - 1 - k)
                self.e_rows = (row >= k + 1) & (row < 2 * HALF - 1 - k)
            self.flag = flags[step] == 1
            self.cut = counts[step] * SHIFT

        def keep(self, p):
            slot = slot_of(p)
            fresh = self.flag & (slot < self.cut) & (slot >= self.cut - SHIFT)
            return jnp.where(fresh, 0.0, 1.0).astype(F32)

        def y_up(self, v):
            v = pltpu.roll(v, 7, 0)
            return v * up_cut if self.shifted else v

        def y_down(self, v, face_no, p):
            v = pltpu.roll(v, 1, 0)
            if self.shifted:
                v = v * down_cut
            if self.use_face:
                v = jnp.where(row == 0, face[face_no, p - HALF], v)
            return v

        def raw_e(self, p):
            return [self.src[c, p] for c in range(3)]

        def magnetic(self, p, store):
            stay = self.keep(p)
            on_cut = slot_of(p) == lax.rem(self.cut + slots - 1, slots)
            above = jnp.where(on_cut, 0.0, 1.0).astype(F32) * self.keep(p + 1)
            ex, ey, ez = (v * stay for v in self.raw_e(p))
            ux, uy = (self.src[c, p + 1] * above for c in range(2))
            old = [self.src[3 + c, p] for c in range(3)]
            hx, hy, hz = (v * stay for v in old)
            hx = hx - 0.5 * ((self.y_up(ez) - ez) - (uy - ey))
            hy = hy - 0.5 * ((ux - ex) - (x_up(ez) - ez))
            hz = hz - 0.5 * ((x_up(ey) - ey) - (self.y_up(ex) - ex))
            new = [jnp.where(self.h_rows, n, o) for n, o in zip((hx, hy, hz), old)]
            if store:
                for c in range(3):
                    self.dst[3 + c, p - self.off] = new[c]
            return tuple(new)

        def electric(self, p, raw, here, below):
            slot = slot_of(p)
            stay = self.keep(p)
            ex, ey, ez = e = [v * stay for v in raw]
            under = jnp.where(slot == self.cut, 0.0, 1.0).astype(F32)
            hx, hy, hz = here
            bx, by = (v * under for v in below)
            cx = (hz - self.y_down(hz, 1, p)) - (hy - by)
            cy = (hx - bx) - (hz - x_down(hz))
            cz = (hy - x_down(hy)) - (hx - self.y_down(hx, 0, p))
            entered = jnp.full(tile, slot, jnp.int32) < self.cut
            eps, half_sigma, kerr = (
                jnp.where(entered, self.coef_inc[i, p], self.coef[i, p]) for i in range(3)
            )
            permit = eps + kerr * (ex * ex + ey * ey + ez * ez)
            inverse = 1.0 / (permit + half_sigma)
            scale = (permit - half_sigma) * inverse
            half_inverse = 0.5 * inverse
            for c, curl in enumerate((cx, cy, cz)):
                updated = scale * e[c] + half_inverse * curl
                self.dst[c, p - self.off] = jnp.where(self.e_rows, updated, raw[c])

        def upward(self, part):
            k = self.k
            lo = k + 1 if part == 0 else 2 * HALF + 3 + HALF * (part - 1) - k
            hi = 2 * HALF + 3 + HALF * part - k
            if part == 0:
                below = self.magnetic(k, self.dst is self.src)[:2]
            else:
                below = tuple(self.dst[3 + c, lo - 1 - self.off] for c in range(2))

            def plane(p, below):
                raw = self.raw_e(p)
                here = self.magnetic(p, True)
                self.electric(p, raw, here, below)
                return here[:2]

            loop(lo, hi, plane, below)

        def downward(self, part):
            k = self.k
            hi = ext - 2 - k if part == 0 else pz - HALF * part + k
            lo = pz - HALF * (part + 1) + k
            if part == 0:
                above = self.magnetic(hi, True)
            else:
                above = tuple(self.dst[3 + c, hi - self.off] for c in range(3))
            split = part == parts - 1 and self.dst is not self.src

            def plane(p, above, store):
                raw = self.raw_e(p + 1)
                here = self.magnetic(p, store)
                self.electric(p + 1, raw, above, here[:2])
                return here

            end = lo + 1 if split else lo
            above = loop(0, hi - end, lambda i, above: plane(hi - 1 - i, above, True), above)
            if split:
                plane(lo, above, False)

    bounds = [0] + [2 * HALF + HALF * j for j in range(parts - 1)] + [ext]
    up_chunks = [(bounds[j], bounds[j + 1]) for j in range(parts)]
    down_chunks = [(ext - hi, ext - lo) for lo, hi in up_chunks]

    up = []
    at = 0
    levels = [Level(k, k, fa, fa, 0, (ca, cia), False, False) for k in range(HALF)]
    for part, (lo, hi) in enumerate(up_chunks):
        if part == parts - 1:
            for copy in first_hi[1:]:
                copy.wait_recv()
        for level in levels:
            level.upward(part)
        base = at

        def pack_up(p, carry):
            for c in range(3):
                sb1[base + 3 * (p - lo) + c] = jnp.where(low_rows, half_turn(fa[c, p]), fa[3 + c, p])
            return carry

        loop(lo, hi, pack_up)
        at += 3 * (hi - lo)
        packed = jnp.zeros(tile, F32)
        for j in range(HALF):
            for n, c in enumerate((0, 2)):
                to = 2 * j + n
                moved = pltpu.roll(fa[3 + c, HALF * (part + 1) + j], (to + 8 - (HALF - 1)) % 8, 0)
                packed = jnp.where(row == to, moved, packed)
        sb1[at] = packed
        at += 1
        span = pl.ds(base, at - base)
        up.append(remote(sb1.at[span], rb1.at[span], ydev(1)))
        start(up[-1])

    for copy in ids_up:
        copy.wait_recv()

    def joined(low, own):
        return jnp.where(low_rows, low, half_turn(own))

    def shifted_coefs(i, carry):
        pair = rm[i]
        put(cb, 2 * i, lookup(joined(pair, ma[2 * i])))
        put(cb, 2 * i + 1, lookup(joined(half_turn(pair), ma[2 * i + 1])))
        entry = inc_plane(2 * i)
        pair = ri[entry // 2]
        put(cib, 2 * i, lookup(joined(pair, inc[entry])))
        put(cib, 2 * i + 1, lookup(joined(half_turn(pair), inc[entry + 1])))
        return carry

    loop(0, ext // 2, shifted_coefs, most=2)

    def join_up(part):
        lo, hi = up_chunks[part]
        base = 3 * lo + part
        up[part].wait_recv()

        def join(p, carry):
            for c in range(3):
                got = rb1[base + 3 * (p - lo) + c]
                fb[c, p] = jnp.where(low_rows, got, half_turn(fa[c, p]))
                fb[3 + c, p] = half_turn(jnp.where(low_rows, fa[3 + c, p], got))
            return carry

        loop(lo, hi, join)
        got = rb1[base + 3 * (hi - lo)]
        for j in range(HALF):
            for n in range(2):
                frm = 2 * j + n
                face[n, HALF * part + j] = got if frm == 0 else pltpu.roll(got, 8 - frm, 0)

    levels = [
        Level(k, k, fb, fb if k < HALF - 1 else fc, 0, (cb, cib), True, True) for k in range(HALF)
    ]
    join_up(0)
    for part in range(parts):
        if part < parts - 1:
            join_up(part + 1)
        for level in levels:
            level.upward(part)
        if part == 0:
            zs_lo[...] = fc[:, HALF : 2 * HALF]
            to_hi = remote(zs_lo, fc.at[:, hi_halo], zdev(-1))
            start(to_hi)
    zs_hi[...] = fc[:, pz : pz + HALF]
    to_lo = remote(zs_hi, fc.at[:, lo_halo], zdev(1))
    start(to_lo)
    to_hi.wait_recv()

    down = []
    levels = [Level(HALF + k, k, fc, fc, 0, (cb, cib), False, True) for k in range(HALF)]
    for part, (lo, hi) in enumerate(down_chunks):
        if part == parts - 1:
            to_lo.wait_recv()
        for level in levels:
            level.downward(part)

        def pack_down(p, carry):
            for c in range(3):
                sb2[3 * p + c] = jnp.where(low_rows, fc[c, p], half_turn(fc[3 + c, p]))
            return carry

        loop(lo, hi, pack_down)
        span = pl.ds(3 * lo, 3 * (hi - lo))
        down.append(remote(sb2.at[span], rb2.at[span], ydev(-1)))
        start(down[-1])

    for p in range(pz):
        for n, c in enumerate((0, 2)):
            face[n, p] = pltpu.roll(fc[3 + c, HALF + p], 8 - (HALF - 1), 0) * face_ok

    def join_down(part):
        lo, hi = down_chunks[part]
        down[part].wait_recv()

        def join(p, carry):
            for c in range(3):
                got = rb2[3 * p + c]
                fb[c, p] = half_turn(jnp.where(low_rows, got, fc[c, p]))
                fb[3 + c, p] = jnp.where(low_rows, half_turn(fc[3 + c, p]), got)
            return carry

        loop(lo, hi, join)

    levels = []
    for k in range(HALF):
        last = k == HALF - 1
        levels.append(Level(HALF + k, k, fb, fo if last else fb, HALF if last else 0, (ca, cia), True, False))
    crossing = lax.rem(g, nz_dev // 2) < 2
    results = []

    def start_results(copies, now):
        @pl.when(now)
        def _():
            for copy in copies:
                copy.start()

    join_down(0)
    for part in range(parts):
        if part < parts - 1:
            join_down(part + 1)
        for level in levels:
            level.downward(part)
        done = pl.ds(pz - HALF * (part + 1), HALF)
        results += [
            remote(fo.at[:, done], out.at[:, done], zdev(-2)),
        ]
        start_results(results[-1:], jnp.logical_not(crossing))
    start_results(results, crossing)
    for copy in results:
        copy.wait_recv()
    for copy in started + results:
        copy.wait_send()


def body(electric, magnetic, material, incoming, shift_flags, eps_table, sigma_table, kerr_table):
    _, pz, py, nx = electric.shape
    ext = pz + 2 * HALF
    n_inc = incoming.shape[0]
    tiles = 3 * ext + pz // HALF

    def buf(*dims, dtype=F32):
        return pltpu.VMEM((*dims, py, nx), dtype)

    ids = jnp.int32
    fields = pl.pallas_call(
        kernel,
        out_shape=jax.ShapeDtypeStruct((6, pz, py, nx), F32),
        in_specs=[pl.BlockSpec(memory_space=pltpu.HBM)] * 8,
        out_specs=pl.BlockSpec(memory_space=pltpu.HBM),
        scratch_shapes=[
            pltpu.SMEM(shift_flags.shape, ids),
            *[pltpu.SMEM(t.shape, F32) for t in (eps_table, sigma_table, kerr_table)],
            buf(n_inc, dtype=ids),
            buf(6, ext), buf(6, ext), buf(6, ext), buf(6, pz),
            buf(3, ext), buf(3, ext), buf(3, ext), buf(3, ext),
            buf(ext, dtype=ids), buf(2, pz), buf(6, HALF), buf(6, HALF),
            buf(ext // 2, dtype=ids), buf(ext // 2, dtype=ids),
            buf(n_inc // 2, dtype=ids), buf(n_inc // 2, dtype=ids),
            buf(tiles), buf(tiles), buf(3 * ext), buf(3 * ext),
            pltpu.SemaphoreType.DMA((30,)),
            pltpu.SemaphoreType.DMA((30,)),
            pltpu.SemaphoreType.DMA((8,)),
        ],
        compiler_params=pltpu.CompilerParams(
            collective_id=0, has_side_effects=True, vmem_limit_bytes=67_000_000
        ),
        name="window_steps",
    )(shift_flags, eps_table, sigma_table, kerr_table, electric, magnetic, material, incoming)
    return fields[:3], fields[3:]


def solution(mesh):
    return jax.shard_map(
        body,
        mesh=mesh,
        in_specs=(
            P(None, "gz", "gy", None),
            P(None, "gz", "gy", None),
            P("gz", "gy", None),
            P(None, "gy", None),
            P(),
            P(),
            P(),
            P(),
        ),
        out_specs=(P(None, "gz", "gy", None), P(None, "gz", "gy", None)),
        check_vma=False,
    )
```

```python
import jax
import jax.numpy as jnp
from jax import lax
from jax.experimental import pallas as pl
from jax.experimental.pallas import tpu as pltpu
from jax.sharding import PartitionSpec as P

STEPS = 8
SHIFT = 8
HALF = 4
MESH = pl.DeviceIdType.MESH
F32 = jnp.float32


def kernel(
    flags_in, eps_in, sig_in, ker_in, e_in, h_in, mat_in, inc_in,
    out,
    flags, eps_t, sig_t, ker_t, inc, fa, fb, fc, fo, ca, cia, cb, cib, ma, face, zs_lo, zs_hi,
    sm, rm, si, ri, sb1, rb1, sb2, rb2, ss, rs, ls,
):
    nz_dev = lax.axis_size("gz")
    ny_dev = lax.axis_size("gy")
    g = lax.axis_index("gz")
    y = lax.axis_index("gy")
    pz = e_in.shape[1]
    nx = e_in.shape[3]
    slots = nz_dev * pz
    ext = pz + 2 * HALF
    tile = (8, nx)
    parts = pz // HALF

    def zdev(d):
        return (lax.rem(g + d + nz_dev, nz_dev), y)

    def ydev(d):
        return (g, lax.rem(y + d + ny_dev, ny_dev))

    barrier = pltpu.get_barrier_semaphore()
    partners = [zdev(1), zdev(-1), ydev(1), ydev(-1), zdev(2), zdev(-2)]
    for dev in partners:
        pl.semaphore_signal(barrier, inc=1, device_id=dev, device_id_type=MESH)

    row = lax.broadcasted_iota(jnp.int32, tile, 0)
    lane = lax.broadcasted_iota(jnp.int32, tile, 1)
    low_rows = row < HALF
    first_lane = lane == 0
    last_lane = lane == nx - 1
    at_edge = y == 0
    up_cut = jnp.where((row == HALF - 1) & at_edge, 0.0, 1.0).astype(F32)
    down_cut = jnp.where((row == HALF) & at_edge, 0.0, 1.0).astype(F32)
    face_ok = jnp.where(at_edge, 0.0, 1.0).astype(F32)

    def half_turn(v):
        return pltpu.roll(v, HALF, 0)

    sem_count = [0]

    def remote(src, dst, dev):
        n = sem_count[0]
        sem_count[0] += 1
        return pltpu.make_async_remote_copy(
            src, dst, ss.at[n], rs.at[n], device_id=dev, device_id_type=MESH
        )

    started = []

    def start(*copies):
        for copy in copies:
            copy.start()
            started.append(copy)

    def loop(lo, hi, step_fn, carry=0, most=6):
        n = hi - lo
        unroll = max(d for d in range(1, most + 1) if n % d == 0)
        return lax.fori_loop(lo, hi, step_fn, carry, unroll=unroll)

    def pack_ids(dst, src, i):
        dst[i] = jnp.where(low_rows, half_turn(src[2 * i]), src[2 * i + 1])

    top = pl.ds(pz - HALF, HALF)
    bottom = pl.ds(0, HALF)
    lo_halo = pl.ds(0, HALF)
    hi_halo = pl.ds(HALF + pz, HALF)
    own = pl.ds(HALF, pz)
    fields = [(e_in, 0), (h_in, 3)]
    inputs = [
        (inc_in, inc),
        (mat_in, ma.at[own]),
        (flags_in, flags),
        (eps_in, eps_t),
        (sig_in, sig_t),
        (ker_in, ker_t),
    ] + [(ref, fa.at[pl.ds(c, 3), own]) for ref, c in fields]
    inputs = [pltpu.make_async_copy(src, dst, ls.at[i]) for i, (src, dst) in enumerate(inputs)]
    for copy in inputs:
        copy.start()

    first_lo = [remote(mat_in.at[top], ma.at[lo_halo], zdev(1))] + [
        remote(ref.at[:, top], fa.at[pl.ds(c, 3), lo_halo], zdev(1)) for ref, c in fields
    ]
    first_hi = [remote(mat_in.at[bottom], ma.at[hi_halo], zdev(-1))] + [
        remote(ref.at[:, bottom], fa.at[pl.ds(c, 3), hi_halo], zdev(-1)) for ref, c in fields
    ]

    pl.semaphore_wait(barrier, len(partners))
    start(*first_lo, *first_hi)

    for copy in inputs:
        copy.wait()
    half_ids = HALF // 2
    own_ids = pl.ds(half_ids, pz // 2)
    for i in range(pz // 2):
        pack_ids(sm, ma, half_ids + i)
    for i in range(inc.shape[0] // 2):
        pack_ids(si, inc, i)
    ids_up = [remote(sm.at[own_ids], rm.at[own_ids], ydev(1)), remote(si, ri, ydev(1))]
    start(*ids_up)

    def lookup(ids):
        out = [jnp.zeros(tile, F32) for _ in range(3)]
        for t in range(eps_t.shape[0]):
            here = ids == t
            for i, tab in enumerate((eps_t, sig_t, ker_t)):
                out[i] = jnp.where(here, tab[t], out[i])
        return out[0], 0.5 * out[1], out[2]

    def slot_of(p):
        return lax.rem(g * pz - HALF + p + slots, slots)

    def put(ref, p, values):
        for i in range(3):
            ref[i, p] = values[i]

    def inc_plane(p):
        return lax.rem(slot_of(p), inc.shape[0])

    def own_incoming(p, carry):
        put(cia, p, lookup(inc[inc_plane(p)]))
        return carry

    def own_material(p, carry):
        put(ca, p, lookup(ma[p]))
        return carry

    loop(HALF, HALF + pz, own_material, most=4)
    loop(0, ext, own_incoming, most=4)

    for copy in first_lo + first_hi[:1]:
        copy.wait_recv()
    for at in (0, ext // 2 - half_ids):
        for i in range(half_ids):
            pack_ids(sm, ma, at + i)
        ends = pl.ds(at, half_ids)
        ids_up.append(remote(sm.at[ends], rm.at[ends], ydev(1)))
    start(*ids_up[2:])
    loop(0, HALF, own_material, most=4)
    loop(HALF + pz, ext, own_material, most=4)

    counts = []
    total = jnp.int32(0)
    for s in range(STEPS):
        total = total + flags[s]
        counts.append(total)

    def x_up(v):
        return jnp.where(last_lane, 0.0, pltpu.roll(v, nx - 1, 1))

    def x_down(v):
        return jnp.where(first_lane, 0.0, pltpu.roll(v, 1, 1))

    class Level:
        def __init__(self, step, k, src, dst, off, coefs, inverted, shifted):
            self.k, self.src, self.dst, self.off = k, src, dst, off
            self.coef, self.coef_inc = coefs
            self.shifted = shifted
            self.use_face = inverted and k == HALF - 1
            if inverted:
                self.h_rows = (row >= HALF - 1 - k) & (row < HALF + k)
                self.e_rows = (row >= HALF - 1 - k) & (row < HALF + 1 + k)
            else:
                self.h_rows = (row >= k) & (row < 2 * HALF - 1 - k)
                self.e_rows = (row >= k + 1) & (row < 2 * HALF - 1 - k)
            self.flag = flags[step] == 1
            self.cut = counts[step] * SHIFT

        def keep(self, p):
            slot = slot_of(p)
            fresh = self.flag & (slot < self.cut) & (slot >= self.cut - SHIFT)
            return jnp.where(fresh, 0.0, 1.0).astype(F32)

        def y_up(self, v):
            v = pltpu.roll(v, 7, 0)
            return v * up_cut if self.shifted else v

        def y_down(self, v, face_no, p):
            v = pltpu.roll(v, 1, 0)
            if self.shifted:
                v = v * down_cut
            if self.use_face:
                v = jnp.where(row == 0, face[face_no, p - HALF], v)
            return v

        def raw_e(self, p):
            return [self.src[c, p] for c in range(3)]

        def magnetic(self, p, store):
            stay = self.keep(p)
            on_cut = slot_of(p) == lax.rem(self.cut + slots - 1, slots)
            above = jnp.where(on_cut, 0.0, 1.0).astype(F32) * self.keep(p + 1)
            ex, ey, ez = (v * stay for v in self.raw_e(p))
            ux, uy = (self.src[c, p + 1] * above for c in range(2))
            old = [self.src[3 + c, p] for c in range(3)]
            hx, hy, hz = (v * stay for v in old)
            hx = hx - 0.5 * ((self.y_up(ez) - ez) - (uy - ey))
            hy = hy - 0.5 * ((ux - ex) - (x_up(ez) - ez))
            hz = hz - 0.5 * ((x_up(ey) - ey) - (self.y_up(ex) - ex))
            new = [jnp.where(self.h_rows, n, o) for n, o in zip((hx, hy, hz), old)]
            if store:
                for c in range(3):
                    self.dst[3 + c, p - self.off] = new[c]
            return tuple(new)

        def electric(self, p, raw, here, below):
            slot = slot_of(p)
            stay = self.keep(p)
            ex, ey, ez = e = [v * stay for v in raw]
            under = jnp.where(slot == self.cut, 0.0, 1.0).astype(F32)
            hx, hy, hz = here
            bx, by = (v * under for v in below)
            cx = (hz - self.y_down(hz, 1, p)) - (hy - by)
            cy = (hx - bx) - (hz - x_down(hz))
            cz = (hy - x_down(hy)) - (hx - self.y_down(hx, 0, p))
            entered = jnp.full(tile, slot, jnp.int32) < self.cut
            eps, half_sigma, kerr = (
                jnp.where(entered, self.coef_inc[i, p], self.coef[i, p]) for i in range(3)
            )
            permit = eps + kerr * (ex * ex + ey * ey + ez * ez)
            inverse = 1.0 / (permit + half_sigma)
            scale = (permit - half_sigma) * inverse
            half_inverse = 0.5 * inverse
            for c, curl in enumerate((cx, cy, cz)):
                updated = scale * e[c] + half_inverse * curl
                self.dst[c, p - self.off] = jnp.where(self.e_rows, updated, raw[c])

        def upward(self, part):
            k = self.k
            lo = k + 1 if part == 0 else 2 * HALF + 3 + HALF * (part - 1) - k
            hi = 2 * HALF + 3 + HALF * part - k
            if part == 0:
                below = self.magnetic(k, self.dst is self.src)[:2]
            else:
                below = tuple(self.dst[3 + c, lo - 1 - self.off] for c in range(2))

            def plane(p, below):
                raw = self.raw_e(p)
                here = self.magnetic(p, True)
                self.electric(p, raw, here, below)
                return here[:2]

            loop(lo, hi, plane, below)

        def downward(self, part):
            k = self.k
            hi = ext - 2 - k if part == 0 else pz - HALF * part + k
            lo = pz - HALF * (part + 1) + k
            if part == 0:
                above = self.magnetic(hi, True)
            else:
                above = tuple(self.dst[3 + c, hi - self.off] for c in range(3))
            split = part == parts - 1 and self.dst is not self.src

            def plane(p, above, store):
                raw = self.raw_e(p + 1)
                here = self.magnetic(p, store)
                self.electric(p + 1, raw, above, here[:2])
                return here

            end = lo + 1 if split else lo
            above = loop(0, hi - end, lambda i, above: plane(hi - 1 - i, above, True), above)
            if split:
                plane(lo, above, False)

    bounds = [0] + [HALF * j for j in range(2, parts + 2)] + [ext]
    up_chunks = [(bounds[j], bounds[j + 1]) for j in range(parts + 1)]
    down_chunks = [(ext - hi, ext - lo) for lo, hi in up_chunks]
    down_chunks[-2:] = [(0, 2 * HALF)]

    up = []
    at = 0
    levels = [Level(k, k, fa, fa, 0, (ca, cia), False, False) for k in range(HALF)]
    for chunk, (lo, hi) in enumerate(up_chunks):
        if chunk == parts - 1:
            for copy in first_hi[1:]:
                copy.wait_recv()
        if chunk < parts:
            for level in levels:
                level.upward(chunk)
        base = at

        def pack_up(p, carry):
            for c in range(3):
                sb1[base + 3 * (p - lo) + c] = jnp.where(low_rows, half_turn(fa[c, p]), fa[3 + c, p])
            return carry

        loop(lo, hi, pack_up)
        at += 3 * (hi - lo)
        if chunk < parts:
            packed = jnp.zeros(tile, F32)
            for j in range(HALF):
                for n, c in enumerate((0, 2)):
                    to = 2 * j + n
                    moved = pltpu.roll(fa[3 + c, HALF * (chunk + 1) + j], (to + 8 - (HALF - 1)) % 8, 0)
                    packed = jnp.where(row == to, moved, packed)
            sb1[at] = packed
            at += 1
        span = pl.ds(base, at - base)
        up.append(remote(sb1.at[span], rb1.at[span], ydev(1)))
        start(up[-1])

    for copy in ids_up:
        copy.wait_recv()

    def joined(low, own):
        return jnp.where(low_rows, low, half_turn(own))

    def shifted_coefs(i, carry):
        pair = rm[i]
        put(cb, 2 * i, lookup(joined(pair, ma[2 * i])))
        put(cb, 2 * i + 1, lookup(joined(half_turn(pair), ma[2 * i + 1])))
        entry = inc_plane(2 * i)
        pair = ri[entry // 2]
        put(cib, 2 * i, lookup(joined(pair, inc[entry])))
        put(cib, 2 * i + 1, lookup(joined(half_turn(pair), inc[entry + 1])))
        return carry

    loop(0, ext // 2, shifted_coefs, most=2)

    def join_up(part):
        lo, hi = up_chunks[part]
        base = 3 * lo + part
        up[part].wait_recv()

        def join(p, carry):
            for c in range(3):
                got = rb1[base + 3 * (p - lo) + c]
                fb[c, p] = jnp.where(low_rows, got, half_turn(fa[c, p]))
                fb[3 + c, p] = half_turn(jnp.where(low_rows, fa[3 + c, p], got))
            return carry

        loop(lo, hi, join)
        if part == parts:
            return
        got = rb1[base + 3 * (hi - lo)]
        for j in range(HALF):
            for n in range(2):
                frm = 2 * j + n
                face[n, HALF * part + j] = got if frm == 0 else pltpu.roll(got, 8 - frm, 0)

    levels = [
        Level(k, k, fb, fb if k < HALF - 1 else fc, 0, (cb, cib), True, True) for k in range(HALF)
    ]
    join_up(0)
    for part in range(parts):
        join_up(part + 1)
        for level in levels:
            level.upward(part)
        if part == 0:
            zs_lo[...] = fc[:, HALF : 2 * HALF]
            to_hi = remote(zs_lo, fc.at[:, hi_halo], zdev(-1))
            start(to_hi)
    zs_hi[...] = fc[:, pz : pz + HALF]
    to_lo = remote(zs_hi, fc.at[:, lo_halo], zdev(1))
    start(to_lo)
    to_hi.wait_recv()

    down = []
    levels = [Level(HALF + k, k, fc, fc, 0, (cb, cib), False, True) for k in range(HALF)]
    for chunk, (lo, hi) in enumerate(down_chunks):
        if chunk == parts - 1:
            to_lo.wait_recv()
        if chunk < parts:
            for level in levels:
                level.downward(chunk)

        def pack_down(p, carry):
            for c in range(3):
                sb2[3 * p + c] = jnp.where(low_rows, fc[c, p], half_turn(fc[3 + c, p]))
            return carry

        loop(lo, hi, pack_down)
        span = pl.ds(3 * lo, 3 * (hi - lo))
        down.append(remote(sb2.at[span], rb2.at[span], ydev(-1)))
        start(down[-1])

    for p in range(pz):
        for n, c in enumerate((0, 2)):
            face[n, p] = pltpu.roll(fc[3 + c, HALF + p], 8 - (HALF - 1), 0) * face_ok

    def join_down(part):
        lo, hi = down_chunks[part]
        down[part].wait_recv()

        def join(p, carry):
            for c in range(3):
                got = rb2[3 * p + c]
                fb[c, p] = half_turn(jnp.where(low_rows, got, fc[c, p]))
                fb[3 + c, p] = jnp.where(low_rows, half_turn(fc[3 + c, p]), got)
            return carry

        loop(lo, hi, join)

    levels = []
    for k in range(HALF):
        last = k == HALF - 1
        levels.append(Level(HALF + k, k, fb, fo if last else fb, HALF if last else 0, (ca, cia), True, False))
    crossing = lax.rem(g, nz_dev // 2) < 2
    results = []

    def start_results(copies, now):
        @pl.when(now)
        def _():
            for copy in copies:
                copy.start()

    join_down(0)
    for part in range(parts):
        if part < parts - 1:
            join_down(part + 1)
        for level in levels:
            level.downward(part)
        done = pl.ds(pz - HALF * (part + 1), HALF)
        results += [
            remote(fo.at[:, done], out.at[:, done], zdev(-2)),
        ]
        start_results(results[-1:], jnp.logical_not(crossing))
    for copy in results[:2]:
        copy.wait_recv()
    start_results(results, crossing)
    for copy in results[2:]:
        copy.wait_recv()
    for copy in started + results:
        copy.wait_send()


def body(electric, magnetic, material, incoming, shift_flags, eps_table, sigma_table, kerr_table):
    _, pz, py, nx = electric.shape
    ext = pz + 2 * HALF
    n_inc = incoming.shape[0]
    tiles = 3 * ext + pz // HALF

    def buf(*dims, dtype=F32):
        return pltpu.VMEM((*dims, py, nx), dtype)

    ids = jnp.int32
    fields = pl.pallas_call(
        kernel,
        out_shape=jax.ShapeDtypeStruct((6, pz, py, nx), F32),
        in_specs=[pl.BlockSpec(memory_space=pltpu.HBM)] * 8,
        out_specs=pl.BlockSpec(memory_space=pltpu.HBM),
        scratch_shapes=[
            pltpu.SMEM(shift_flags.shape, ids),
            *[pltpu.SMEM(t.shape, F32) for t in (eps_table, sigma_table, kerr_table)],
            buf(n_inc, dtype=ids),
            buf(6, ext), buf(6, ext), buf(6, ext), buf(6, pz),
            buf(3, ext), buf(3, ext), buf(3, ext), buf(3, ext),
            buf(ext, dtype=ids), buf(2, pz), buf(6, HALF), buf(6, HALF),
            buf(ext // 2, dtype=ids), buf(ext // 2, dtype=ids),
            buf(n_inc // 2, dtype=ids), buf(n_inc // 2, dtype=ids),
            buf(tiles), buf(tiles), buf(3 * ext), buf(3 * ext),
            pltpu.SemaphoreType.DMA((30,)),
            pltpu.SemaphoreType.DMA((30,)),
            pltpu.SemaphoreType.DMA((8,)),
        ],
        compiler_params=pltpu.CompilerParams(
            collective_id=0, has_side_effects=True, vmem_limit_bytes=67_000_000
        ),
        name="window_steps",
    )(shift_flags, eps_table, sigma_table, kerr_table, electric, magnetic, material, incoming)
    return fields[:3], fields[3:]


def solution(mesh):
    return jax.shard_map(
        body,
        mesh=mesh,
        in_specs=(
            P(None, "gz", "gy", None),
            P(None, "gz", "gy", None),
            P("gz", "gy", None),
            P(None, "gy", None),
            P(),
            P(),
            P(),
            P(),
        ),
        out_specs=(P(None, "gz", "gy", None), P(None, "gz", "gy", None)),
        check_vma=False,
    )
```
